32 devices in a mesh: section: 2 (over core), expert: 4 (over z), dp: 4 (over y, x).
Axes of the slice: x: 2, y: 2, z: 4, core: 2. Of those that a mesh axis runs over, the one named last changes fastest.
Arguments:
- inputs: bfloat16 [2080, 768], P(('expert', 'dp')), may hold values from -6 to 6
- cotangent: float32 [2080, 768], P(('expert', 'dp')), may hold values from -6 to 6
- expert_ids: int32 [2, 2080, 2], P('section', ('expert', 'dp')), may hold values from 0 to 3, all different within a row; in each aligned block of 65 rows (0 to 64, 65 to 129, ..., all dimensions but the last counted through in order) at most 41 rows name the same one
- gain_one: float32 [2, 768], P('section'), may hold values from 0.5 to 1.5
- shift_one: float32 [2, 768], P('section'), may hold values from -3 to 3
- w_qkv: bfloat16 [2, 768, 2304], P('section'), may hold values from -1 to 1
- w_out: bfloat16 [2, 768, 768], P('section'), may hold values from -0.625 to 0.625
- gain_two: float32 [2, 768], P('section'), may hold values from 0.5 to 1.5
- shift_two: float32 [2, 768], P('section'), may hold values from -3 to 3
- w_router: bfloat16 [2, 768, 4], P('section'), may hold values from -4 to 4
- w_in: bfloat16 [2, 4, 768, 3072], P('section', 'expert'), may hold values from -0.21875 to 0.21875
- b_in: float32 [2, 4, 3072], P('section', 'expert'), may hold values from -3 to 3
- w_exit: bfloat16 [2, 4, 3072, 768], P('section', 'expert'), may hold values from -0.875 to 0.875
- b_exit: float32 [2, 4, 768], P('section', 'expert'), may hold values from -3 to 3
Outputs:
- acts: bfloat16 [2, 2080, 768], P('section', ('expert', 'dp'))
- input_grads: float32 [2, 2080, 768], P('section', ('expert', 'dp'))
- grad_gain_one: float32 [2, 768], P('section', ('expert', 'dp'))
- grad_shift_one: float32 [2, 768], P('section', ('expert', 'dp'))
- grad_w_qkv: float32 [2, 768, 2304], P('section', ('expert', 'dp'))
- grad_w_out: float32 [2, 768, 768], P('section', ('expert', 'dp'))
- grad_gain_two: float32 [2, 768], P('section', ('expert', 'dp'))
- grad_shift_two: float32 [2, 768], P('section', ('expert', 'dp'))
- grad_w_router: float32 [2, 768, 4], P('section', ('expert', 'dp'))
- grad_w_in: float32 [2, 4, 768, 3072], P('section', 'expert', None, 'dp')
- grad_b_in: float32 [2, 4, 3072], P('section', 'expert', 'dp')
- grad_w_exit: float32 [2, 4, 3072, 768], P('section', 'expert', 'dp')
- grad_b_exit: float32 [2, 4, 768], P('section', 'expert', 'dp')
The draws below stay inside these ranges and needn't reach their ends.
Inputs may be any that keep to these rules, and one draw needn't show every extreme that they name: `expert_ids`: the two entries of a row differ. In each aligned block of 65 rows of one block index (one device's micro-batch), no expert is named by more than 41 rows; in some blocks one is named by exactly 41.
All inputs are finite; a program needn't handle non-finite values.
Results may differ from the reference program's by a relative error of at most 0.03.
Values may be sent and summed in bfloat16 or wider, within the bound.
No kernel may reach another device: no remote copies, remote signals or barrier semaphores. Data moves between devices by JAX's collectives and lax.ppermute only.
A program may use at most 192 MiB of HBM per device.

```python
import math
import jax
import jax.numpy as jnp
import numpy as np
from jax import lax

D = 768
HEADS = 12
HEAD_DIM = 64
FF = 3072
IMAGES_MB = 1
SEQ = 65
EXPERTS = 4
CAP = 41
TOKENS = 2080


def draw_inputs(key, part):
    sample = jax.random.normal(jax.random.fold_in(key, 11), (TOKENS, D), jnp.float32)
    return jnp.clip(sample, -6.0, 6.0).astype(jnp.bfloat16)


def draw_w_qkv(key, part):
    sample = jax.random.normal(jax.random.fold_in(key, 21), (2, D, 3 * D), jnp.float32)
    return jnp.clip(sample * D ** (-0.5), -1.0, 1.0).astype(jnp.bfloat16)


def draw_w_router(key, part):
    sample = jax.random.normal(jax.random.fold_in(key, 31), (2, D, EXPERTS), jnp.float32) * (1.5 * D ** (-0.5))
    return jnp.clip(sample, -4.0, 4.0).astype(jnp.bfloat16)


def shard_levels(key, dims, shards, low, top_value):
    level, own = 1.0, jax.random.fold_in(key, 6)
    for axis_at, parts in shards:
        heights = jnp.exp(jax.random.uniform(jax.random.fold_in(own, axis_at), (parts,), jnp.float32, low / len(shards), top_value / len(shards)))
        level = level * jnp.repeat(heights, dims[axis_at] // parts).reshape([-1 if axis == axis_at else 1 for axis in range(len(dims))])
    return level


def assign_block(rng, own, number, rows, count, top, bound, skew):
    sequence = jax.random.permutation(rng, count)
    packed, usual = load_shares(count, rows * top, bound, skew, True), load_shares(count, rows * top, bound, skew, False)
    places = jnp.arange(count)

    def named(lengths, rotation):
        used = int((lengths > 0).sum())
        fixed = max(1, used // 4)
        shifted = fixed + (places - fixed + rotation * (used - fixed)) % max(1, count - fixed)
        return jnp.zeros((count,), jnp.int32).at[sequence[jnp.where(places < fixed, places, shifted)]].set(jnp.asarray(lengths, jnp.int32))

    lengths = jnp.where(number % 4 == 0, named(packed, number // 4), named(usual, number - number // 4 - 1))
    mixed = jax.random.permutation(jax.random.fold_in(own, 3), count)
    source_of, sink = mixed[0:count // 2 * 2:2], mixed[1:count // 2 * 2:2]
    slack = jnp.minimum(lengths[source_of] - 1, bound - lengths[sink]) // 2
    slack = jnp.where((source_of == sequence[0]) | (sink == sequence[0]) | (lengths[sink] == 0), 0, jnp.maximum(slack, 0))
    shifted = jax.random.randint(jax.random.fold_in(own, 4), (count // 2,), 0, 1 << 20) % (slack + 1)
    lengths = lengths.at[source_of].add(-shifted).at[sink].add(shifted)
    members = jnp.searchsorted(jnp.cumsum(lengths), jnp.arange(rows * top), side="right").astype(jnp.int32)
    table = members.reshape(top, rows).T
    table = table[jax.random.permutation(jax.random.fold_in(own, 1), rows)]
    rotation = jax.random.randint(jax.random.fold_in(own, 2), (rows, 1), 0, top)
    return jnp.take_along_axis(table, (jnp.arange(top)[None, :] + rotation) % top, axis=1)


def load_shares(number_of, total, bound, slope, full):
    weights = [(1 << 20) // math.isqrt(rank ** slope) + 1 for rank in range(1, number_of + 1)]
    largest = bound if full else min(bound, max(-(-total // number_of), total * weights[0] // sum(weights)))
    least = 1 if total - largest >= number_of - 1 else 0
    holding, surplus = [largest] + [least] * (number_of - 1), total - largest - least * (number_of - 1)
    while surplus > 0:
        candidates = [i for i in range(1, number_of) if holding[i] < largest] or [i for i in range(1, number_of) if holding[i] < bound]
        whole, budget = sum([weights[i] for i in candidates]), surplus
        for i in candidates:
            extra = min(bound - holding[i], max(1, budget * weights[i] // whole), surplus)
            holding[i] = holding[i] + extra
            surplus = surplus - extra
    return np.array(holding)


def normal_values(stream_key, shape, scale, most, shards=(), held_as=jnp.bfloat16):
    level = shard_levels(stream_key, shape, shards, -0.22, 0.18) if shards else 1.0
    drawn = jax.random.normal(stream_key, shape, jnp.float32) * scale * level
    return jnp.minimum(jnp.maximum(drawn, -most), most).astype(held_as)


def setup_inputs(seed: int = 0) -> dict:
    key_list = jax.random.split(jax.random.key(seed), 15)
    inputs = draw_inputs(jax.random.fold_in(key_list[14], 71), 0)
    cotangent = normal_values(key_list[1], (TOKENS, D), 1.0, 6.0, ((0, 16),), jnp.float32)
    expert_ids_keys = jax.random.split(jax.random.fold_in(key_list[2], 1), 2 * TOKENS // (IMAGES_MB * SEQ))
    expert_ids_turns = jax.random.permutation(jax.random.fold_in(key_list[2], 3), 2 * TOKENS // (IMAGES_MB * SEQ))
    expert_ids = jax.vmap(lambda own, number: assign_block(jax.random.fold_in(key_list[2], 2), own, number, IMAGES_MB * SEQ, EXPERTS, 2, CAP, 2))(expert_ids_keys, expert_ids_turns).reshape((2, TOKENS, 2))
    gain_one = jnp.clip(1.0 + 0.1 * jax.random.normal(key_list[3], (2, D), jnp.float32), 0.5, 1.5)
    shift_one = normal_values(key_list[4], (2, D), 0.3, 3.0, ((0, 2),), jnp.float32)
    w_qkv = draw_w_qkv(jax.random.fold_in(key_list[14], 71), 0)
    w_out = normal_values(key_list[6], (2, D, D), (D // 8) ** -0.5, 0.625, ((0, 2),))
    gain_two = jnp.clip(1.0 + 0.1 * jax.random.normal(key_list[7], (2, D), jnp.float32), 0.5, 1.5)
    shift_two = normal_values(key_list[8], (2, D), 0.3, 3.0, ((0, 2),), jnp.float32)
    w_router = draw_w_router(jax.random.fold_in(key_list[14], 71), 0)
    w_in = normal_values(key_list[10], (2, EXPERTS, D, FF), D ** -0.5, 0.21875, ((0, 2), (1, 4)))
    b_in = normal_values(key_list[11], (2, EXPERTS, FF), 0.5, 3.0, ((0, 2), (1, 4)), jnp.float32)
    w_exit = normal_values(key_list[12], (2, EXPERTS, FF, D), (FF // 64) ** -0.5, 0.875, ((0, 2), (1, 4)))
    b_exit = normal_values(key_list[13], (2, EXPERTS, D), 0.5, 3.0, ((0, 2), (1, 4)), jnp.float32)
    return dict(inputs=inputs, cotangent=cotangent, expert_ids=expert_ids, gain_one=gain_one, shift_one=shift_one, w_qkv=w_qkv, w_out=w_out, gain_two=gain_two, shift_two=shift_two, w_router=w_router, w_in=w_in, b_in=b_in, w_exit=w_exit, b_exit=b_exit)


EPSILON = 1e-06
ROOT_HALF = 0.7071067811865476
DENSITY = 0.3989422804014327

def rounded(entries):
    return lax.optimization_barrier(entries.astype(jnp.bfloat16))

def gelu_value(entries):
    return 0.5 * entries * (1.0 + lax.erf(entries * ROOT_HALF))

def gelu_slope(entries):
    return 0.5 * (1.0 + lax.erf(entries * ROOT_HALF)) + entries * jnp.exp(-0.5 * entries * entries) * DENSITY

def layer_norm(values):
    centre = lax.optimization_barrier(jnp.mean(values, axis=-1, keepdims=True))
    spread = lax.optimization_barrier(jnp.mean(jnp.square(values - centre), axis=-1, keepdims=True))
    inverse = lax.rsqrt(spread + EPSILON)
    return ((values - centre) * inverse, inverse)

def norm_back(grad_normed, normed, inverse):
    first_mean = lax.optimization_barrier(jnp.mean(grad_normed, axis=-1, keepdims=True))
    second_mean = lax.optimization_barrier(jnp.mean(grad_normed * normed, axis=-1, keepdims=True))
    return inverse * (grad_normed - first_mean - normed * second_mean)

def softmax_rows(logits):
    largest = lax.optimization_barrier(jnp.max(logits, axis=-1, keepdims=True))
    weights = jnp.exp(logits - largest)
    return weights / lax.optimization_barrier(jnp.sum(weights, axis=-1, keepdims=True))

def slot_table(choices, experts):
    count_rows = choices.shape[0]
    expert_hits = (choices[:, :, None] == jnp.arange(experts, dtype=jnp.int32)).astype(jnp.int32)
    ordered = jnp.swapaxes(expert_hits, 0, 1).reshape(2 * count_rows, experts)
    before = jnp.cumsum(ordered, axis=0) - ordered
    places = lax.optimization_barrier(jnp.sum(before * ordered, axis=-1)).reshape(2, count_rows)
    return jnp.swapaxes(places, 0, 1).astype(jnp.int32)

def attention_forward(qkv_half):
    images = qkv_half.shape[0] // SEQ
    pieces = qkv_half.astype(jnp.float32).reshape(images, SEQ, 3, HEADS, HEAD_DIM)
    scores = jnp.einsum('ishd,ithd->ihst', pieces[:, :, 0], pieces[:, :, 1]) * HEAD_DIM ** (-0.5)
    largest = lax.optimization_barrier(jnp.max(scores, axis=-1, keepdims=True))
    log_total = largest + jnp.log(lax.optimization_barrier(jnp.sum(jnp.exp(scores - largest), axis=-1, keepdims=True)))
    probs_half = rounded(jnp.exp(scores - log_total)).astype(jnp.float32)
    mixed_heads = jnp.einsum('ihst,ithd->ishd', probs_half, pieces[:, :, 2])
    return (rounded(mixed_heads.reshape(images * SEQ, D)), log_total)

def attention_backward(qkv_half, log_total, grad_mixed):
    images = qkv_half.shape[0] // SEQ
    pieces = qkv_half.astype(jnp.float32).reshape(images, SEQ, 3, HEADS, HEAD_DIM)
    queries = pieces[:, :, 0]
    keys_part = pieces[:, :, 1]
    values_part = pieces[:, :, 2]
    grad_heads = grad_mixed.astype(jnp.float32).reshape(images, SEQ, HEADS, HEAD_DIM)
    scores = jnp.einsum('ishd,ithd->ihst', queries, keys_part) * HEAD_DIM ** (-0.5)
    attn_probs = jnp.exp(scores - log_total)
    probs_half = rounded(attn_probs).astype(jnp.float32)
    grad_values = jnp.einsum('ihst,ishd->ithd', probs_half, grad_heads)
    grad_probs = jnp.einsum('ishd,ithd->ihst', grad_heads, values_part)
    grad_scores = attn_probs * (grad_probs - lax.optimization_barrier(jnp.sum(attn_probs * grad_probs, axis=-1, keepdims=True))) * HEAD_DIM ** (-0.5)
    grad_scores = rounded(grad_scores).astype(jnp.float32)
    grad_queries = jnp.einsum('ihst,ithd->ishd', grad_scores, keys_part)
    grad_keys = jnp.einsum('ihst,ishd->ithd', grad_scores, queries)
    stacked = jnp.stack([grad_queries, grad_keys, grad_values], axis=2)
    return rounded(stacked.reshape(images * SEQ, 3 * D))

def block_forward(source, params, choices):
    gain_a, shift_a, weight_qkv, weight_out, gain_b, shift_b, weight_router, weight_in, bias_in, weight_exit, bias_exit = params
    values = source.astype(jnp.float32)
    normed_one, inverse_one = layer_norm(values)
    attn_in = rounded(normed_one * gain_a + shift_a)
    qkv_half = rounded(jnp.dot(attn_in, weight_qkv, preferred_element_type=jnp.float32))
    mixed_heads, log_total = attention_forward(qkv_half)
    residual = values + jnp.dot(mixed_heads, weight_out, preferred_element_type=jnp.float32)
    normed_two, inverse_two = layer_norm(residual)
    routed = rounded(normed_two * gain_b + shift_b)
    router_probs = softmax_rows(jnp.dot(routed, weight_router, preferred_element_type=jnp.float32))
    expert_hits = (choices[:, :, None] == jnp.arange(EXPERTS, dtype=jnp.int32)).astype(jnp.float32)
    gate_values = lax.optimization_barrier(jnp.sum(expert_hits * router_probs[:, None, :], axis=-1))
    block_rows = IMAGES_MB * SEQ
    blocks = TOKENS // block_rows
    places = jax.vmap(lambda block_ids: slot_table(block_ids, EXPERTS))(choices.reshape(blocks, block_rows, 2)).reshape(TOKENS, 2)
    owners = jnp.broadcast_to((jnp.arange(TOKENS, dtype=jnp.int32) // block_rows)[:, None], (TOKENS, 2)).astype(jnp.int32)
    spread_rows = jnp.broadcast_to(routed[:, None, :], (TOKENS, 2, D))
    buffers = jnp.zeros((EXPERTS, blocks, CAP, D), jnp.bfloat16).at[choices, owners, places].set(spread_rows)

    def expert_forward(operands):
        rows_in, first_w, first_b, second_w, second_b = operands
        flat_rows = rows_in.reshape(blocks * CAP, D)
        hidden = jnp.dot(flat_rows, first_w, preferred_element_type=jnp.float32) + first_b
        active = rounded(gelu_value(hidden))
        result = rounded(jnp.dot(active, second_w, preferred_element_type=jnp.float32) + second_b)
        return (result.reshape(blocks, CAP, D), hidden)
    outputs, hiddens = lax.map(expert_forward, (buffers, weight_in, bias_in, weight_exit, bias_exit))
    returned = outputs[choices, owners, places]
    final_sum = residual + lax.optimization_barrier(jnp.sum(gate_values[:, :, None] * returned.astype(jnp.float32), axis=1))
    kept_state = (normed_one, inverse_one, attn_in, qkv_half, mixed_heads, log_total, normed_two, inverse_two, routed, router_probs, expert_hits, gate_values, owners, places, buffers, hiddens, returned)
    return (rounded(final_sum), kept_state)

def block_backward(grad_final, params, choices, kept_state):
    gain_a, shift_a, weight_qkv, weight_out, gain_b, shift_b, weight_router, weight_in, bias_in, weight_exit, bias_exit = params
    normed_one, inverse_one, attn_in, qkv_half, mixed_heads, log_total, normed_two, inverse_two, routed, router_probs, expert_hits, gate_values, owners, places, buffers, hiddens, returned = kept_state
    grad_out = rounded(gate_values[:, :, None] * grad_final[:, None, :])
    grad_gates = lax.optimization_barrier(jnp.sum(grad_final[:, None, :] * returned.astype(jnp.float32), axis=-1))
    grad_buffers = jnp.zeros_like(buffers).at[choices, owners, places].set(grad_out)

    def expert_backward(operands):
        rows_in, grads_in, hidden, first_w, second_w = operands
        flat_rows = rows_in.reshape(-1, D)
        flat_grads = grads_in.reshape(-1, D)
        active = rounded(gelu_value(hidden))
        grad_second = jnp.dot(active.T, flat_grads, preferred_element_type=jnp.float32)
        grad_second_b = lax.optimization_barrier(jnp.sum(flat_grads.astype(jnp.float32), axis=0))
        grad_hidden = jnp.dot(flat_grads, second_w.T, preferred_element_type=jnp.float32) * gelu_slope(hidden)
        grad_first_b = lax.optimization_barrier(jnp.sum(grad_hidden, axis=0))
        hidden_half = rounded(grad_hidden)
        grad_first = jnp.dot(flat_rows.T, hidden_half, preferred_element_type=jnp.float32)
        grad_rows = rounded(jnp.dot(hidden_half, first_w.T, preferred_element_type=jnp.float32))
        return (grad_first, grad_first_b, grad_second, grad_second_b, grad_rows.reshape(rows_in.shape))
    grad_w_in, grad_b_in, grad_w_exit, grad_b_exit, grad_rows = lax.map(expert_backward, (buffers, grad_buffers, hiddens, weight_in, weight_exit))
    back_rows = grad_rows[choices, owners, places]
    grad_probs = lax.optimization_barrier(jnp.sum(expert_hits * grad_gates[:, :, None], axis=1))
    grad_logits = rounded(router_probs * (grad_probs - lax.optimization_barrier(jnp.sum(router_probs * grad_probs, axis=-1, keepdims=True))))
    grad_w_router = jnp.dot(routed.T, grad_logits, preferred_element_type=jnp.float32)
    grad_routed = lax.optimization_barrier(jnp.sum(back_rows.astype(jnp.float32), axis=1)) + jnp.dot(grad_logits, weight_router.T, preferred_element_type=jnp.float32)
    grad_gain_two = lax.optimization_barrier(jnp.sum(grad_routed * normed_two, axis=0))
    grad_shift_two = lax.optimization_barrier(jnp.sum(grad_routed, axis=0))
    grad_residual = grad_final + norm_back(grad_routed * gain_b, normed_two, inverse_two)
    residual_half = rounded(grad_residual)
    grad_w_out = jnp.dot(mixed_heads.T, residual_half, preferred_element_type=jnp.float32)
    grad_mixed = rounded(jnp.dot(residual_half, weight_out.T, preferred_element_type=jnp.float32))
    grad_qkv = attention_backward(qkv_half, log_total, grad_mixed)
    grad_w_qkv = jnp.dot(attn_in.T, grad_qkv, preferred_element_type=jnp.float32)
    grad_attn = jnp.dot(grad_qkv, weight_qkv.T, preferred_element_type=jnp.float32)
    grad_gain_one = lax.optimization_barrier(jnp.sum(grad_attn * normed_one, axis=0))
    grad_shift_one = lax.optimization_barrier(jnp.sum(grad_attn, axis=0))
    grad_source = grad_residual + norm_back(grad_attn * gain_a, normed_one, inverse_one)
    return (grad_source, (grad_gain_one, grad_shift_one, grad_w_qkv, grad_w_out, grad_gain_two, grad_shift_two, grad_w_router, grad_w_in, grad_b_in, grad_w_exit, grad_b_exit))

def reference(inputs, cotangent, expert_ids, gain_one, shift_one, w_qkv, w_out, gain_two, shift_two, w_router, w_in, b_in, w_exit, b_exit):
    weights = (gain_one, shift_one, w_qkv, w_out, gain_two, shift_two, w_router, w_in, b_in, w_exit, b_exit)
    first_params = tuple((weight[0] for weight in weights))
    second_params = tuple((weight[1] for weight in weights))
    first_out, first_state = block_forward(inputs, first_params, expert_ids[0])
    second_out, second_state = block_forward(first_out, second_params, expert_ids[1])
    second_grad, second_weights = block_backward(cotangent, second_params, expert_ids[1], second_state)
    first_grad, first_weights = block_backward(second_grad, first_params, expert_ids[0], first_state)
    stacked = tuple((jnp.stack([first_grad_w, second_grad_w]) for first_grad_w, second_grad_w in zip(first_weights, second_weights)))
    acts = jnp.stack([first_out, second_out])
    input_grads = jnp.stack([first_grad, second_grad])
    return (acts, input_grads, stacked[0], stacked[1], stacked[2], stacked[3], stacked[4], stacked[5], stacked[6], stacked[7], stacked[8], stacked[9], stacked[10])
```

```python
import jax
import jax.numpy as jnp
from jax import lax
from jax.sharding import PartitionSpec as P

D = 768
HEADS = 12
HEAD_DIM = 64
SEQ = 65
EPSILON = 1e-06
ROOT_HALF = 0.7071067811865476
DENSITY = 0.3989422804014327
F32 = jnp.float32
BF16 = jnp.bfloat16


def moved(array, axis, pairs, sections):
    length = lax.axis_size(axis)
    perm = [(s * length + i, s * length + j) for s in sections for i, j in pairs]
    return lax.ppermute(array, ("section", axis), perm)


def rotated(array, by, sections):
    length = lax.axis_size("expert")
    return moved(array, "expert", [(i, (i + by) % length) for i in range(length)], sections)


def crossed(array, mask, sections):
    length = lax.axis_size("dp")
    return moved(array, "dp", [(i, i ^ mask) for i in range(length)], sections)


def gelu_value(entries):
    return 0.5 * entries * (1.0 + lax.erf(entries * ROOT_HALF))


def gelu_slope(entries):
    return (
        0.5 * (1.0 + lax.erf(entries * ROOT_HALF))
        + entries * jnp.exp(-0.5 * entries * entries) * DENSITY
    )


def layer_norm(values):
    centre = jnp.mean(values, axis=-1, keepdims=True)
    spread = jnp.mean(jnp.square(values - centre), axis=-1, keepdims=True)
    inverse = lax.rsqrt(spread + EPSILON)
    return ((values - centre) * inverse, inverse)


def norm_back(grad_normed, normed, inverse):
    first_mean = jnp.mean(grad_normed, axis=-1, keepdims=True)
    second_mean = jnp.mean(grad_normed * normed, axis=-1, keepdims=True)
    return inverse * (grad_normed - first_mean - normed * second_mean)


def softmax_rows(logits):
    largest = jnp.max(logits, axis=-1, keepdims=True)
    weights = jnp.exp(logits - largest)
    return weights / jnp.sum(weights, axis=-1, keepdims=True)


def mul(left, right):
    return jnp.dot(left, right, preferred_element_type=F32)


def mul_tn(left, right):
    return lax.dot_general(left, right, (((0,), (0,)), ((), ())), preferred_element_type=F32)


def mul_nt(left, right):
    return lax.dot_general(left, right, (((1,), (1,)), ((), ())), preferred_element_type=F32)


def attention_forward(qkv_half):
    images = qkv_half.shape[0] // SEQ
    pieces = qkv_half.reshape(images, SEQ, 3, HEADS, HEAD_DIM)
    scores = jnp.einsum(
        "ishd,ithd->ihst", pieces[:, :, 0], pieces[:, :, 1], preferred_element_type=F32
    ) * HEAD_DIM ** (-0.5)
    largest = jnp.max(scores, axis=-1, keepdims=True)
    log_total = largest + jnp.log(jnp.sum(jnp.exp(scores - largest), axis=-1, keepdims=True))
    probs_half = jnp.exp(scores - log_total).astype(BF16)
    mixed_heads = jnp.einsum(
        "ihst,ithd->ishd", probs_half, pieces[:, :, 2], preferred_element_type=F32
    )
    return (mixed_heads.reshape(images * SEQ, D).astype(BF16), log_total)


def attention_backward(qkv_half, log_total, grad_mixed):
    images = qkv_half.shape[0] // SEQ
    pieces = qkv_half.reshape(images, SEQ, 3, HEADS, HEAD_DIM)
    queries, keys_part, values_part = pieces[:, :, 0], pieces[:, :, 1], pieces[:, :, 2]
    grad_heads = grad_mixed.reshape(images, SEQ, HEADS, HEAD_DIM)
    scores = jnp.einsum(
        "ishd,ithd->ihst", queries, keys_part, preferred_element_type=F32
    ) * HEAD_DIM ** (-0.5)
    attn_probs = jnp.exp(scores - log_total)
    probs_half = attn_probs.astype(BF16)
    grad_values = jnp.einsum("ihst,ishd->ithd", probs_half, grad_heads, preferred_element_type=F32)
    grad_probs = jnp.einsum("ishd,ithd->ihst", grad_heads, values_part, preferred_element_type=F32)
    grad_scores = (
        attn_probs
        * (grad_probs - jnp.sum(attn_probs * grad_probs, axis=-1, keepdims=True))
        * HEAD_DIM ** (-0.5)
    ).astype(BF16)
    grad_queries = jnp.einsum("ihst,ithd->ishd", grad_scores, keys_part, preferred_element_type=F32)
    grad_keys = jnp.einsum("ihst,ishd->ithd", grad_scores, queries, preferred_element_type=F32)
    stacked = jnp.stack([grad_queries, grad_keys, grad_values], axis=2)
    return stacked.reshape(images * SEQ, 3 * D).astype(BF16)


def on_device(
    inputs, cotangent, expert_ids, gain_one, shift_one, w_qkv, w_out, gain_two, shift_two,
    w_router, w_in, b_in, w_exit, b_exit,
):
    tokens = inputs.shape[0]
    n = lax.axis_size("expert")
    peers = lax.axis_size("dp")
    capacity = (tokens // SEQ) * (5 * SEQ // (2 * n) + 1)
    cap = -(-capacity // 8) * 8
    slots = n * cap
    my_dp = lax.axis_index("dp")
    my_expert = lax.axis_index("expert")
    is_first = lax.axis_index("section") == 0
    gain_a, shift_a, weight_qkv, weight_out = gain_one[0], shift_one[0], w_qkv[0], w_out[0]
    gain_b, shift_b, weight_router = gain_two[0], shift_two[0], w_router[0]
    weight_in, bias_in, weight_exit, bias_exit = w_in[0, 0], b_in[0, 0], w_exit[0, 0], b_exit[0, 0]
    choices = expert_ids[0]
    part = weight_in.shape[1] // peers
    heads_part = 3 * D // peers
    out_part = D // peers

    hits = (choices[:, :, None] == jnp.arange(n, dtype=jnp.int32)).astype(F32)
    named = jnp.sum(hits, axis=1)
    earlier = jnp.tril(jnp.ones((tokens, tokens), BF16), -1)
    before = mul(earlier, named.astype(BF16))
    places = jnp.sum(hits * before[:, None, :], axis=-1).astype(jnp.int32)
    spots = jnp.mod(choices - my_expert, n) * cap + places
    selects = [
        (spots[:, k : k + 1] == jnp.arange(slots, dtype=jnp.int32)).astype(BF16) for k in range(2)
    ]
    select_both = selects[0] + selects[1]

    def to_experts(rows, sections):
        blocks = [rows[r * cap : (r + 1) * cap] for r in range(n)]
        return jnp.concatenate(
            [blocks[0]] + [rotated(blocks[r], r, sections) for r in range(1, n)], axis=0
        )

    def from_experts(rows, sections):
        blocks = [rows[r * cap : (r + 1) * cap] for r in range(n)]
        return jnp.concatenate(
            [blocks[0]] + [rotated(blocks[r], -r, sections) for r in range(1, n)], axis=0
        )

    def gathered(rows, sections):
        return [rows] + [crossed(rows, m, sections) for m in range(1, peers)]

    def dealt(rows, width, sections):
        pieces = [
            lax.dynamic_slice_in_dim(rows, (my_dp ^ m) * width, width, 1) for m in range(peers)
        ]
        return [pieces[0]] + [crossed(pieces[m], m, sections) for m in range(1, peers)]

    def forward(source, sections):
        values = source.astype(F32)
        normed_one, inverse_one = layer_norm(values)
        attn_in = (normed_one * gain_a + shift_a).astype(BF16)
        qkv_half = mul(attn_in, weight_qkv).astype(BF16)
        mixed_heads, log_total = attention_forward(qkv_half)
        residual = values + mul(mixed_heads, weight_out)
        normed_two, inverse_two = layer_norm(residual)
        routed = (normed_two * gain_b + shift_b).astype(BF16)
        router_probs = softmax_rows(mul(routed, weight_router))
        gates = jnp.sum(hits * router_probs[:, None, :], axis=-1)
        received = to_experts(mul_tn(select_both, routed).astype(BF16), sections)
        hidden = mul(received, weight_in) + bias_in
        active = gelu_value(hidden).astype(BF16)
        result = (mul(active, weight_exit) + bias_exit).astype(BF16)
        back = from_experts(result, sections)
        returned = [mul(s, back) for s in selects]
        final = residual + gates[:, 0:1] * returned[0] + gates[:, 1:2] * returned[1]
        state = (
            normed_one, inverse_one, attn_in, qkv_half, mixed_heads, log_total, normed_two,
            inverse_two, routed, router_probs, gates, returned, received, hidden, active,
        )
        return final.astype(BF16), state

    def backward(grad_final, state, sections):
        (
            normed_one, inverse_one, attn_in, qkv_half, mixed_heads, log_total, normed_two,
            inverse_two, routed, router_probs, gates, returned, received, hidden, active,
        ) = state
        grad_out = [(gates[:, k : k + 1] * grad_final).astype(BF16) for k in range(2)]
        grad_gates = jnp.stack([jnp.sum(grad_final * returned[k], axis=-1) for k in range(2)], 1)
        grad_buffers = mul_tn(selects[0], grad_out[0]) + mul_tn(selects[1], grad_out[1])
        grad_received = to_experts(grad_buffers.astype(BF16), sections)
        grad_hidden = mul_nt(grad_received, weight_exit) * gelu_slope(hidden)
        hidden_half = grad_hidden.astype(BF16)
        grad_rows = mul_nt(hidden_half, weight_in).astype(BF16)
        grad_back = from_experts(grad_rows, sections)
        back_rows = mul(select_both, grad_back)
        grad_probs = jnp.sum(hits * grad_gates[:, :, None], axis=1)
        grad_logits = (
            router_probs * (grad_probs - jnp.sum(router_probs * grad_probs, axis=-1, keepdims=True))
        ).astype(BF16)
        part_router = mul_tn(routed, grad_logits)
        grad_routed = back_rows + mul_nt(grad_logits, weight_router)
        part_gain_two = jnp.sum(grad_routed * normed_two, axis=0)
        part_shift_two = jnp.sum(grad_routed, axis=0)
        grad_residual = grad_final + norm_back(grad_routed * gain_b, normed_two, inverse_two)
        residual_half = grad_residual.astype(BF16)
        grad_mixed = mul_nt(residual_half, weight_out).astype(BF16)
        grad_qkv = attention_backward(qkv_half, log_total, grad_mixed)
        grad_attn = mul_nt(grad_qkv, weight_qkv)
        part_gain_one = jnp.sum(grad_attn * normed_one, axis=0)
        part_shift_one = jnp.sum(grad_attn, axis=0)
        grad_source = grad_residual + norm_back(grad_attn * gain_a, normed_one, inverse_one)
        small = jnp.concatenate(
            [part_gain_one[:, None], part_shift_one[:, None], part_gain_two[:, None],
             part_shift_two[:, None], part_router], axis=1
        )
        return grad_source, small, grad_received, hidden_half, residual_half, grad_qkv

    first_out, first_state = forward(inputs, (0,))
    second_out, second_state = forward(
        lax.ppermute(first_out, "section", [(0, 1)]), (1,)
    )
    both = (0, 1)
    rows_kept = jnp.where(is_first, first_state[12], second_state[12])
    active_kept = jnp.where(is_first, first_state[14], second_state[14])
    attn_kept = jnp.where(is_first, first_state[2], second_state[2])
    mixed_kept = jnp.where(is_first, first_state[4], second_state[4])
    rows_all = gathered(rows_kept, both)
    active_all = dealt(active_kept, part, both)
    attn_all = gathered(attn_kept, both)
    mixed_all = gathered(mixed_kept, both)

    def dense(residual_half, grad_qkv, small, sections):
        qkv_all = dealt(grad_qkv, heads_part, sections)
        res_all = dealt(residual_half, out_part, sections)
        small_all = gathered(small.astype(BF16), sections)
        w_qkv_part = sum(mul_tn(a, g) for a, g in zip(attn_all, qkv_all))
        w_out_part = sum(mul_tn(a, g) for a, g in zip(mixed_all, res_all))
        small_part = sum(s.astype(F32) for s in small_all)
        pad = -small_part.shape[1] % 128
        small_part = jnp.pad(small_part, ((0, 0), (0, pad))) * (1.0 / peers)
        joined = jnp.concatenate([w_qkv_part, w_out_part, small_part], axis=1).astype(BF16)
        block = D // n
        pieces = [
            lax.dynamic_slice_in_dim(joined, jnp.mod(my_expert + r, n) * block, block, 0)
            for r in range(n)
        ]
        own = sum(
            [pieces[0].astype(F32)]
            + [rotated(pieces[r], r, sections).astype(F32) for r in range(1, n)]
        )
        own = own.astype(BF16)
        row = block // peers
        bits = [lax.dynamic_slice_in_dim(own, (my_dp ^ m) * row, row, 0) for m in range(peers)]
        return [bits[0]] + [crossed(bits[m], m, sections) for m in range(1, peers)]

    second_grad, second_small, second_rec, second_hh, second_res, second_gq = backward(
        cotangent, second_state, (1,)
    )
    carried = lax.ppermute(second_grad.astype(BF16), "section", [(1, 0)]).astype(F32)
    second_dense = dense(second_res, second_gq, second_small, (1,))
    second_rec_all = gathered(second_rec, (1,))
    second_hh_all = dealt(second_hh, part, (1,))
    first_grad, first_small, first_rec, first_hh, first_res, first_gq = backward(
        carried, first_state, (0,)
    )
    first_rec_all = gathered(first_rec, (0,))
    first_hh_all = dealt(first_hh, part, (0,))
    first_dense = dense(first_res, first_gq, first_small, (0,))

    def pick(a, b):
        return [jnp.where(is_first, x, y) for x, y in zip(a, b)]

    rec_all = pick(first_rec_all, second_rec_all)
    hh_all = pick(first_hh_all, second_hh_all)
    final_dense = pick(first_dense, second_dense)
    grad_w_in = sum(mul_tn(a, g) for a, g in zip(rows_all, hh_all))
    grad_b_in = sum(jnp.sum(g.astype(F32), axis=0) for g in hh_all)
    grad_w_exit = sum(mul_tn(a, g) for a, g in zip(active_all, rec_all))
    grad_b_exit = lax.dynamic_slice_in_dim(
        sum(jnp.sum(g.astype(F32), axis=0) for g in rec_all), my_dp * out_part, out_part, 0
    )

    stacked = jnp.stack(final_dense)
    ordered = jnp.take(stacked, jnp.arange(peers) ^ my_dp, axis=0).astype(F32)
    out_qkv = jnp.swapaxes(ordered[:, :, :heads_part], 0, 1).reshape(-1, 3 * D)
    out_out = jnp.swapaxes(ordered[:, :, heads_part : heads_part + out_part], 0, 1).reshape(-1, D)
    smalls = jnp.sum(ordered[:, :, heads_part + out_part :], axis=0)
    acts = jnp.where(is_first, first_out, second_out)
    input_grads = jnp.where(is_first, first_grad, second_grad)
    return (
        acts[None], input_grads[None], smalls[None, :, 0], smalls[None, :, 1], out_qkv[None],
        out_out[None], smalls[None, :, 2], smalls[None, :, 3], smalls[None, :, 4 : 4 + n],
        grad_w_in[None, None], grad_b_in[None, None], grad_w_exit[None, None],
        grad_b_exit[None, None],
    )


def solution(mesh):
    both = ("expert", "dp")
    return jax.shard_map(
        on_device,
        mesh=mesh,
        in_specs=(
            P(both, None), P(both, None), P("section", both, None), P("section", None),
            P("section", None), P("section", None, None), P("section", None, None),
            P("section", None), P("section", None), P("section", None, None),
            P("section", "expert", None, None), P("section", "expert", None),
            P("section", "expert", None, None), P("section", "expert", None),
        ),
        out_specs=(
            P("section", both, None), P("section", both, None), P("section", both),
            P("section", both), P("section", both, None), P("section", both, None),
            P("section", both), P("section", both), P("section", both, None),
            P("section", "expert", None, "dp"), P("section", "expert", "dp"),
            P("section", "expert", "dp", None), P("section", "expert", "dp"),
        ),
        check_vma=False,
    )
```

```python
import functools

import jax
import jax.numpy as jnp
from jax import lax
from jax.experimental import pallas as pl
from jax.experimental.pallas import tpu as pltpu
from jax.sharding import PartitionSpec as P

D = 768
HEADS = 12
HEAD_DIM = 64
SEQ = 65
EPSILON = 1e-06
ROOT_HALF = 0.7071067811865476
DENSITY = 0.3989422804014327
F32 = jnp.float32
BF16 = jnp.bfloat16


def moved(array, axis, pairs, sections):
    length = lax.axis_size(axis)
    perm = [(s * length + i, s * length + j) for s in sections for i, j in pairs]
    return lax.ppermute(array, ("section", axis), perm)


def rotated(array, by, sections):
    length = lax.axis_size("expert")
    return moved(array, "expert", [(i, (i + by) % length) for i in range(length)], sections)


def crossed(array, mask, sections):
    length = lax.axis_size("dp")
    return moved(array, "dp", [(i, i ^ mask) for i in range(length)], sections)


def gelu_value(entries):
    return 0.5 * entries * (1.0 + lax.erf(entries * ROOT_HALF))


def gelu_slope(entries):
    return (
        0.5 * (1.0 + lax.erf(entries * ROOT_HALF))
        + entries * jnp.exp(-0.5 * entries * entries) * DENSITY
    )


def layer_norm(values):
    centre = jnp.mean(values, axis=-1, keepdims=True)
    spread = jnp.mean(jnp.square(values - centre), axis=-1, keepdims=True)
    inverse = lax.rsqrt(spread + EPSILON)
    return ((values - centre) * inverse, inverse)


def norm_back(grad_normed, normed, inverse):
    first_mean = jnp.mean(grad_normed, axis=-1, keepdims=True)
    second_mean = jnp.mean(grad_normed * normed, axis=-1, keepdims=True)
    return inverse * (grad_normed - first_mean - normed * second_mean)


def softmax_rows(logits):
    largest = jnp.max(logits, axis=-1, keepdims=True)
    weights = jnp.exp(logits - largest)
    return weights / jnp.sum(weights, axis=-1, keepdims=True)


def mul(left, right):
    return jnp.dot(left, right, preferred_element_type=F32)


def mul_tn(left, right):
    return lax.dot_general(left, right, (((0,), (0,)), ((), ())), preferred_element_type=F32)


def mul_nt(left, right):
    return lax.dot_general(left, right, (((1,), (1,)), ((), ())), preferred_element_type=F32)


def image_mask(tokens):
    rows = lax.broadcasted_iota(jnp.int32, (tokens, tokens), 0)
    cols = lax.broadcasted_iota(jnp.int32, (tokens, tokens), 1)
    same = None
    for i in range(tokens // SEQ):
        low, high = i * SEQ, (i + 1) * SEQ
        inside = (rows >= low) & (rows < high) & (cols >= low) & (cols < high)
        same = inside if same is None else same | inside
    return same


def head_lanes(tokens):
    return lax.broadcasted_iota(jnp.int32, (tokens, 2 * HEAD_DIM), 1) < HEAD_DIM


def gate_of(probs, choices, k):
    lanes = lax.broadcasted_iota(jnp.int32, probs.shape, 1)
    return jnp.sum(jnp.where(lanes == choices[:, k : k + 1], probs, 0.0), axis=-1, keepdims=True)


def make_selects(n, cap, choices, turned, select_o):
    tokens = choices.shape[0]
    lanes = lax.broadcasted_iota(jnp.int32, (tokens, 128), 1)
    mine = [lanes == choices[:, k : k + 1] for k in range(2)]
    named = jnp.where(mine[0] | mine[1], 1.0, 0.0).astype(BF16)
    row = lax.broadcasted_iota(jnp.int32, (tokens, tokens), 0)
    col = lax.broadcasted_iota(jnp.int32, (tokens, tokens), 1)
    before = mul(jnp.where(col < row, 1.0, 0.0).astype(BF16), named)
    slot = lax.broadcasted_iota(jnp.int32, (tokens, n * cap), 1)
    found = []
    for k in range(2):
        place = jnp.sum(jnp.where(mine[k], before, 0.0), axis=-1, keepdims=True)
        spot = turned[:, k : k + 1] * cap + place.astype(jnp.int32)
        found.append(slot == spot)
        select_o[k] = jnp.where(found[k], 1.0, 0.0).astype(BF16)
    select_o[2] = jnp.where(found[0] | found[1], 1.0, 0.0).astype(BF16)


def forward_body(
    n, cap, source, gain_a, shift_a, weight_qkv, weight_out, gain_b, shift_b, weight_router,
    choices, turned, attn_in_o, qkv_o, mixed_o, log_o, residual_o, probs_o, buffers_o, select_o,
):
    tokens = source.shape[0]
    filler = jnp.zeros((attn_in_o.shape[0] - tokens, D), BF16)
    attn_in_o[tokens:, :] = filler
    mixed_o[tokens:, :] = filler
    values = source[...].astype(F32)
    normed_one, _ = layer_norm(values)
    attn_in = (normed_one * gain_a[...] + shift_a[...]).astype(BF16)
    attn_in_o[:tokens, :] = attn_in
    qkv_o[...] = mul(attn_in, weight_qkv[...]).astype(BF16)
    same = image_mask(tokens)
    left = head_lanes(tokens)
    log_lanes = lax.broadcasted_iota(jnp.int32, (tokens, 128), 1)
    logs = jnp.zeros((tokens, 128), F32)
    for pair in range(HEADS // 2):
        at = pair * 2 * HEAD_DIM
        q = qkv_o[:, at : at + 2 * HEAD_DIM]
        k = qkv_o[:, D + at : D + at + 2 * HEAD_DIM]
        v = qkv_o[:, 2 * D + at : 2 * D + at + 2 * HEAD_DIM]
        outs = []
        for side in range(2):
            keep = left if side == 0 else jnp.logical_not(left)
            q_side = jnp.where(keep, q, jnp.zeros_like(q))
            scores = mul_nt(q_side, k) * HEAD_DIM ** (-0.5)
            scores = jnp.where(same, scores, -1e30)
            largest = jnp.max(scores, axis=-1, keepdims=True)
            total = largest + jnp.log(jnp.sum(jnp.exp(scores - largest), axis=-1, keepdims=True))
            probs = jnp.exp(scores - total).astype(BF16)
            logs = jnp.where(log_lanes == 2 * pair + side, total, logs)
            outs.append(mul(probs, v))
        mixed_o[:tokens, at : at + 2 * HEAD_DIM] = jnp.where(left, outs[0], outs[1]).astype(BF16)
    log_o[...] = logs
    residual = values + mul(mixed_o[:tokens, :], weight_out[...])
    residual_o[...] = residual
    normed_two, _ = layer_norm(residual)
    routed = (normed_two * gain_b[...] + shift_b[...]).astype(BF16)
    logits = mul(routed, weight_router[...])
    lanes = lax.broadcasted_iota(jnp.int32, logits.shape, 1)
    logits = jnp.where(lanes < n, logits, -1e30)
    probs_o[...] = softmax_rows(logits)
    make_selects(n, cap, choices, turned, select_o)
    buffers_o[...] = mul_tn(select_o[2], routed).astype(BF16)


def combine_body(residual, probs, choices, select, back, final_o):
    gate_a = gate_of(probs[...], choices[...], 0)
    gate_b = gate_of(probs[...], choices[...], 1)
    returned_a = mul(select[0], back[...])
    returned_b = mul(select[1], back[...])
    final_o[...] = (residual[...] + (gate_a * returned_a + gate_b * returned_b)).astype(BF16)


def dispatch_back_body(
    grad_final, probs, choices, select, back,
    buffers_o, logits_o,
):
    grads = grad_final[...].astype(F32)
    prob = probs[...]
    lanes = lax.broadcasted_iota(jnp.int32, prob.shape, 1)
    buffers = None
    grad_probs = jnp.zeros_like(prob)
    for k in range(2):
        mine = lanes == choices[:, k : k + 1]
        gate = jnp.sum(jnp.where(mine, prob, 0.0), axis=-1, keepdims=True)
        added = mul_tn(select[k], (gate * grads).astype(BF16))
        buffers = added if buffers is None else buffers + added
        returned = mul(select[k], back[...])
        grad_gate = jnp.sum(grads * returned, axis=-1, keepdims=True)
        grad_probs = grad_probs + jnp.where(mine, grad_gate, 0.0)
    buffers_o[...] = buffers.astype(BF16)
    logits_o[...] = (
        prob * (grad_probs - jnp.sum(prob * grad_probs, axis=-1, keepdims=True))
    ).astype(BF16)


def backward_body(
    grad_final, grad_back, select, grad_logits, weight_router, residual, gain_b, shift_b,
    weight_out, qkv, logs, weight_qkv, source, gain_a,
    grad_source_o, carried_o, dense_o, small_o, grad_qkv_s,
):
    tokens = source.shape[0]
    grads = grad_final[...].astype(F32)
    normed_two, inverse_two = layer_norm(residual[...])
    routed = (normed_two * gain_b[...] + shift_b[...]).astype(BF16)
    logits = grad_logits[...]
    router = mul_tn(logits, routed)
    grad_routed = mul(select[2], grad_back[...]) + mul_nt(logits, weight_router[...])
    gain_two = jnp.sum(grad_routed * normed_two, axis=0, keepdims=True)
    shift_two = jnp.sum(grad_routed, axis=0, keepdims=True)
    grad_residual = grads + norm_back(grad_routed * gain_b[...], normed_two, inverse_two)
    residual_half = grad_residual.astype(BF16)
    dense_o[3, :tokens, :] = residual_half
    for p in range(4):
        dense_o[p, tokens:, :] = jnp.zeros((dense_o.shape[1] - tokens, D), BF16)
    grad_mixed = mul_nt(residual_half, weight_out[...]).astype(BF16)
    same = image_mask(tokens)
    left = head_lanes(tokens)

    def put(p, at, sides):
        value = jnp.where(left, sides[0], sides[1]).astype(BF16)
        dense_o[p, :tokens, at : at + 2 * HEAD_DIM] = value
        grad_qkv_s[:, p * D + at : p * D + at + 2 * HEAD_DIM] = value

    for pair in range(HEADS // 2):
        at = pair * 2 * HEAD_DIM
        q = qkv[:, at : at + 2 * HEAD_DIM]
        k = qkv[:, D + at : D + at + 2 * HEAD_DIM]
        v = qkv[:, 2 * D + at : 2 * D + at + 2 * HEAD_DIM]
        g = grad_mixed[:, at : at + 2 * HEAD_DIM]
        gq, gk, gv = [], [], []
        for side in range(2):
            keep = left if side == 0 else jnp.logical_not(left)
            head = 2 * pair + side
            q_side = jnp.where(keep, q, jnp.zeros_like(q))
            g_side = jnp.where(keep, g, jnp.zeros_like(g))
            scores = mul_nt(q_side, k) * HEAD_DIM ** (-0.5)
            scores = jnp.where(same, scores, -1e30)
            probs = jnp.exp(scores - logs[:, head : head + 1])
            grad_p = mul_nt(g_side, v)
            grad_s = (
                probs
                * (grad_p - jnp.sum(probs * grad_p, axis=-1, keepdims=True))
                * HEAD_DIM ** (-0.5)
            ).astype(BF16)
            gq.append(mul(grad_s, k))
            gk.append(mul_tn(grad_s, q))
            gv.append(mul_tn(probs.astype(BF16), g))
        put(0, at, gq)
        put(1, at, gk)
        put(2, at, gv)
    grad_attn = mul_nt(grad_qkv_s[...], weight_qkv[...])
    normed_one, inverse_one = layer_norm(source[...].astype(F32))
    gain_one = jnp.sum(grad_attn * normed_one, axis=0, keepdims=True)
    shift_one = jnp.sum(grad_attn, axis=0, keepdims=True)
    grad_source = grad_residual + norm_back(grad_attn * gain_a[...], normed_one, inverse_one)
    grad_source_o[...] = grad_source
    carried_o[...] = grad_source.astype(BF16)
    small_o[0:1, :] = gain_one
    small_o[1:2, :] = shift_one
    small_o[2:3, :] = gain_two
    small_o[3:4, :] = shift_two
    small_o[4:8, :] = jnp.zeros((4, D), F32)
    small_o[8:, :] = router[: small_o.shape[0] - 8, :]


def whole(body, name, outs, scratch=()):
    return pl.pallas_call(
        body,
        out_shape=tuple(jax.ShapeDtypeStruct(s, d) for s, d in outs),
        scratch_shapes=list(scratch),
        name=name,
        compiler_params=pltpu.CompilerParams(vmem_limit_bytes=48 * 1024 * 1024),
    )


def on_device(
    inputs, cotangent, expert_ids, gain_one, shift_one, w_qkv, w_out, gain_two, shift_two,
    w_router, w_in, b_in, w_exit, b_exit,
):
    tokens = inputs.shape[0]
    n = lax.axis_size("expert")
    peers = lax.axis_size("dp")
    assert peers == 4
    capacity = (tokens // SEQ) * (5 * SEQ // (2 * n) + 1)
    cap = -(-capacity // 8) * 8
    slots = n * cap
    padded = -(-tokens // 16) * 16
    small_rows = 8 + -(-n // 8) * 8
    my_dp = lax.axis_index("dp")
    my_expert = lax.axis_index("expert")
    is_first = lax.axis_index("section") == 0
    weight_qkv, weight_out = w_qkv[0], w_out[0]
    weight_router = jnp.pad(w_router[0], ((0, 0), (0, 128 - n)))
    weight_in, bias_in, weight_exit, bias_exit = w_in[0, 0], b_in[0, 0], w_exit[0, 0], b_exit[0, 0]
    choices = expert_ids[0]
    turned = jnp.mod(choices - my_expert, n)
    part = weight_in.shape[1] // peers

    def to_experts(rows, sections):
        blocks = [rows[r * cap : (r + 1) * cap] for r in range(n)]
        return jnp.concatenate(
            [blocks[0]] + [rotated(blocks[r], r, sections) for r in range(1, n)], axis=0
        )

    def from_experts(rows, sections):
        blocks = [rows[r * cap : (r + 1) * cap] for r in range(n)]
        return jnp.concatenate(
            [blocks[0]] + [rotated(blocks[r], -r, sections) for r in range(1, n)], axis=0
        )

    def dealt(pieces, sections):
        return [pieces[0]] + [crossed(pieces[m], m, sections) for m in range(1, peers)]

    def columns(rows, m):
        return lax.dynamic_slice_in_dim(rows, (my_dp ^ m) * part, part, 1)

    def forward(source, sections):
        attn_in, qkv, mixed, logs, residual, probs, buffers, select = whole(
            functools.partial(forward_body, n, cap), "forward_attention",
            [((padded, D), BF16), ((tokens, 3 * D), BF16), ((padded, D), BF16),
             ((tokens, 128), F32), ((tokens, D), F32), ((tokens, 128), F32), ((slots, D), BF16),
             ((3, tokens, slots), BF16)],
        )(source, gain_one, shift_one, weight_qkv, weight_out, gain_two, shift_two,
          weight_router, choices, turned)
        received = to_experts(buffers, sections)
        hidden = mul(received, weight_in) + bias_in
        active = gelu_value(hidden).astype(BF16)
        result = (mul(active, weight_exit) + bias_exit).astype(BF16)
        back = from_experts(result, sections)
        (final,) = whole(combine_body, "combine", [((tokens, D), BF16)])(
            residual, probs, choices, select, back
        )
        return final, (source, attn_in, qkv, mixed, logs, residual, probs, select, back,
                       received, hidden, active)

    def backward(grad_final, state, sections):
        (source, _, qkv, _, logs, residual, probs, select, back, _, hidden, _) = state
        buffers, logits = whole(
            dispatch_back_body, "dispatch_back", [((slots, D), BF16), ((tokens, 128), BF16)]
        )(grad_final, probs, choices, select, back)
        grad_received = to_experts(buffers, sections)
        grad_hidden = mul_nt(grad_received, weight_exit) * gelu_slope(hidden)
        hidden_half = grad_hidden.astype(BF16)
        grad_rows = mul_nt(hidden_half, weight_in).astype(BF16)
        grad_back = from_experts(grad_rows, sections)
        grad_source, carried, dense, small = whole(
            backward_body, "backward_attention",
            [((tokens, D), F32), ((tokens, D), BF16), ((4, padded, D), BF16),
             ((small_rows, D), F32)],
            [pltpu.VMEM((tokens, 3 * D), BF16)],
        )(grad_final, grad_back, select, logits, weight_router, residual, gain_two, shift_two,
          weight_out, qkv, logs, weight_qkv, source, gain_one)
        return grad_source, carried, dense, small, grad_received, hidden_half

    def forward_pieces(state):
        attn_in, mixed, received, active = state[1], state[3], state[9], state[11]
        return [
            jnp.concatenate(
                [received, columns(active, m),
                 jnp.where((my_dp ^ m) == 3, mixed, attn_in)], axis=0
            ) for m in range(peers)
        ]

    def backward_pieces(dense, grad_received, hidden_half):
        return [
            jnp.concatenate(
                [grad_received, columns(hidden_half, m),
                 lax.dynamic_index_in_dim(dense, my_dp ^ m, 0, keepdims=False)], axis=0
            ) for m in range(peers)
        ]

    def spread_dense(fore, aft, sections):
        joined = sum(mul_tn(f[2 * slots :], b[2 * slots :]) for f, b in zip(fore, aft))
        joined = joined.astype(BF16)
        block = D // n
        pieces = [
            lax.dynamic_slice_in_dim(joined, jnp.mod(my_expert + r, n) * block, block, 0)
            for r in range(n)
        ]
        return sum(
            [pieces[0].astype(F32)]
            + [rotated(pieces[r], r, sections).astype(F32) for r in range(1, n)]
        )

    first_out, first_state = forward(inputs, (0,))
    arrived = lax.ppermute(first_out, "section", [(0, 1)])
    first_fore = dealt(forward_pieces(first_state), (0,))
    second_out, second_state = forward(arrived, (1,))
    second_grad, carried, second_dense, second_small, second_rec, second_hh = backward(
        cotangent, second_state, (1,)
    )
    handed = lax.ppermute(carried, "section", [(1, 0)])
    fore_pieces, aft_pieces = forward_pieces(second_state), backward_pieces(
        second_dense, second_rec, second_hh
    )
    second_fore = dealt(fore_pieces, (1,))
    second_aft = dealt(aft_pieces, (1,))
    second_own = spread_dense(second_fore, second_aft, (1,))
    first_grad, _, first_dense, first_small, first_rec, first_hh = backward(
        handed, first_state, (0,)
    )
    first_aft = dealt(backward_pieces(first_dense, first_rec, first_hh), (0,))
    first_own = spread_dense(first_fore, first_aft, (0,))

    def pick(a, b):
        return jnp.where(is_first, a, b)

    fore = [pick(a, b) for a, b in zip(first_fore, second_fore)]
    aft = [pick(a, b) for a, b in zip(first_aft, second_aft)]
    grad_w_in = sum(mul_tn(a[:slots], g[slots : 2 * slots]) for a, g in zip(fore, aft))
    grad_b_in = sum(jnp.sum(g[slots : 2 * slots].astype(F32), axis=0) for g in aft)
    grad_w_exit = sum(mul_tn(a[slots : 2 * slots], g[:slots]) for a, g in zip(fore, aft))
    width = D // peers
    grad_b_exit = lax.dynamic_slice_in_dim(
        sum(jnp.sum(g[:slots].astype(F32), axis=0) for g in aft), my_dp * width, width, 0
    )
    own = pick(first_own, second_own).astype(BF16).reshape(peers, D // n // peers, D)
    placed = lax.all_to_all(own, "dp", split_axis=0, concat_axis=0, tiled=True).astype(F32)
    out_qkv = jnp.concatenate([placed[0], placed[1], placed[2]], axis=1)
    small = pick(first_small, second_small).reshape(small_rows, n * peers, -1)
    small = lax.all_to_all(
        jnp.swapaxes(small, 0, 1), ("expert", "dp"), split_axis=0, concat_axis=0, tiled=True
    )
    small = jnp.sum(small, axis=0)
    acts = pick(first_out, second_out)
    input_grads = pick(first_grad, second_grad)
    return (
        acts[None], input_grads[None], small[0:1], small[1:2], out_qkv[None],
        placed[3][None], small[2:3], small[3:4], small[8 : 8 + n].T[None],
        grad_w_in[None, None], grad_b_in[None, None], grad_w_exit[None, None],
        grad_b_exit[None, None],
    )


def solution(mesh):
    both = ("expert", "dp")
    return jax.shard_map(
        on_device,
        mesh=mesh,
        in_specs=(
            P(both, None), P(both, None), P("section", both, None), P("section", None),
            P("section", None), P("section", None, None), P("section", None, None),
            P("section", None), P("section", None), P("section", None, None),
            P("section", "expert", None, None), P("section", "expert", None),
            P("section", "expert", None, None), P("section", "expert", None),
        ),
        out_specs=(
            P("section", both, None), P("section", both, None), P("section", both),
            P("section", both), P("section", both, None), P("section", both, None),
            P("section", both), P("section", both), P("section", both, None),
            P("section", "expert", None, "dp"), P("section", "expert", "dp"),
            P("section", "expert", "dp", None), P("section", "expert", "dp"),
        ),
        check_vma=False,
    )
```
